128 devices in a mesh: seq: 128 (over z, y, x, core).
Axes of the slice: x: 4, y: 4, z: 4, core: 2. Of those that a mesh axis runs over, the one named last changes fastest.
Arguments:
- queries: bfloat16 [32768, 3200], P('seq'), may hold values from -6 to 6
- keys: bfloat16 [32768, 3200], P('seq'), may hold values from -6 to 6
- values: bfloat16 [32768, 3200], P('seq'), may hold values from -6 to 6
- img_height: int32 [1026], replicated, may hold values from 0 to 56, as said below
- img_width: int32 [1026], replicated, may hold values from 0 to 32, as said below
- norm_gain: float32 [12800], replicated, may hold values from 0.5 to 1.5
- norm_bias: float32 [12800], replicated, may hold values from -3 to 3
Outputs:
- merged: bfloat16 [8192, 12800], P('seq')
The draws below stay inside these ranges and needn't reach their ends.
Inputs may be any that keep to these rules, and one draw needn't show every extreme that they name: Images are packed in slot order without gaps: the products img_height * img_width sum to 32768; heights and widths are even; an image has at most 896 patches and some image has exactly 896; some image is 56 patches high; slots after the last image hold zero rows and zero columns, and there is always at least one such slot. `img_width`: A nonempty image is at most 32 patches wide, and some image is exactly 32 wide.
All inputs are finite; a program needn't handle non-finite values.
Results may differ from the reference program's by a relative error of at most 0.0053.
Values may be sent and summed in bfloat16 or wider, within the bound.
A program may use at most 128 MiB of HBM per device.

```python
import math
import jax
import jax.numpy as jnp
from jax import lax

HEAD_DIM = 128
D = 3200
TOK_DEV = 256
MOST = 896
WMAX = 32
REACH = 4
TOKENS = 32768
MERGED = 8192
NIMG = 1026


def grid_layout(key):
    base = jax.random.fold_in(key, 5)
    first_key, second_key, third_key, fourth_key = jax.random.split(base, 4)
    merged_most = MOST // 4
    merged_wide = WMAX // 2
    merged_narrow = WMAX // 4
    leading_width = merged_narrow + 1
    width_draw = jax.random.randint(first_key, (NIMG,), merged_narrow, merged_wide + 1)
    raw_bits = jax.random.randint(second_key, (NIMG,), 0, 1 << 20)
    forced = jax.random.randint(third_key, (), 1, 5)
    tallest = 1 + (forced + jax.random.randint(fourth_key, (), 0, 3)) % 4
    slot_index = jnp.arange(NIMG, dtype=jnp.int32)

    def place(remain, inputs):
        slot, width_pick, bits_pick = inputs
        width_pick = jnp.where(slot == forced, merged_wide, jnp.where(slot == tallest, merged_narrow, width_pick))
        width_pick = jnp.where(slot == 0, leading_width, width_pick)
        height_pick = 1 + bits_pick % (merged_most // width_pick)
        height_pick = jnp.where(slot == forced, merged_most // merged_wide, height_pick)
        height_pick = jnp.where(slot == tallest, merged_most // merged_narrow, height_pick)
        height_pick = jnp.where(slot == 0, merged_most // leading_width, height_pick)
        taken = jnp.minimum(height_pick, remain // width_pick)
        enough = taken >= 1
        out_height = jnp.where(enough, taken, jnp.where(remain > 0, 1, 0))
        out_width = jnp.where(enough, width_pick, remain)
        return (remain - out_height * out_width, (out_height, out_width))
    start_remain = jnp.array(TOKENS // 4, jnp.int32)
    leftover, shapes = lax.scan(place, start_remain, (slot_index, width_draw, raw_bits))
    return ((2 * shapes[0]).astype(jnp.int32), (2 * shapes[1]).astype(jnp.int32))


def draw_img_height(key, part):
    return grid_layout(key)[0]


def draw_img_width(key, part):
    return grid_layout(key)[1]


def attention_pair(key):
    base = jax.random.fold_in(key, 7)
    query_key, key_key = jax.random.split(base, 2)
    query_field = jnp.clip(jax.random.normal(query_key, (TOKENS, D), jnp.float32), -6.0, 6.0)
    key_field = jnp.clip(jax.random.normal(key_key, (TOKENS, D), jnp.float32), -6.0, 6.0)
    return (query_field, key_field)


def draw_queries(key, part):
    return attention_pair(key)[0].astype(jnp.bfloat16)


def draw_keys(key, part):
    return attention_pair(key)[1].astype(jnp.bfloat16)


def block_levels(rng, extent, shards, low, largest):
    def one(position, shards_of):
        draws = jax.random.uniform(jax.random.fold_in(jax.random.fold_in(rng, 6), position), (shards_of,), jnp.float32, low / len(shards), largest / len(shards))
        return jnp.repeat(jnp.exp(draws), extent[position] // shards_of).reshape((-1,) + (1,) * (len(extent) - position - 1))

    gain = one(*shards[0])
    for cut in shards[1:]:
        gain = gain * one(*cut)
    return gain


def normal_values(key, extent, scale, limit, cuts=(), kind=jnp.bfloat16):
    level = block_levels(key, extent, cuts, -0.22, 0.18) if cuts else 1.0
    entries = jax.random.normal(key, extent, jnp.float32) * scale * level
    return jnp.minimum(jnp.maximum(entries, -limit), limit).astype(kind)


def setup_inputs(seed: int = 0) -> dict:
    arg_keys = jax.random.split(jax.random.key(seed), 8)
    queries = draw_queries(jax.random.fold_in(arg_keys[7], 71), 0)
    keys = draw_keys(jax.random.fold_in(arg_keys[7], 71), 0)
    values = normal_values(arg_keys[2], (TOKENS, D), 1.0, 6.0, ((0, 128),))
    img_height = draw_img_height(jax.random.fold_in(arg_keys[7], 71), 0)
    img_width = draw_img_width(jax.random.fold_in(arg_keys[7], 71), 0)
    norm_gain = jnp.clip(1.0 + 0.1 * jax.random.normal(arg_keys[5], (4 * D,), jnp.float32), 0.5, 1.5)
    norm_bias = normal_values(arg_keys[6], (4 * D,), 0.5, 3.0, (), jnp.float32)
    return {"queries": queries, "keys": keys, "values": values, "img_height": img_height, "img_width": img_width, "norm_gain": norm_gain, "norm_bias": norm_bias}


def image_index(image_ends, positions):
    return jnp.searchsorted(image_ends, positions, side='right').astype(jnp.int32)

def head_attention(query_block, key_window, value_window, allowed):
    softmax_scale = 1.0 / math.sqrt(HEAD_DIM)
    head_count = query_block.shape[1] // HEAD_DIM

    def one_head(head_index, result):
        column = head_index * HEAD_DIM
        q_head = lax.dynamic_slice_in_dim(query_block, column, HEAD_DIM, 1)
        k_head = lax.dynamic_slice_in_dim(key_window, column, HEAD_DIM, 1)
        v_head = lax.dynamic_slice_in_dim(value_window, column, HEAD_DIM, 1)
        scores = lax.dot_general(q_head, k_head, (((1,), (1,)), ((), ())), preferred_element_type=jnp.float32) * softmax_scale
        scores = jnp.where(allowed, scores, -jnp.inf)
        row_max = lax.optimization_barrier(jnp.max(scores, axis=1, keepdims=True))
        weights = jnp.exp(scores - row_max)
        totals = lax.optimization_barrier(jnp.sum(weights, axis=1, keepdims=True))
        weights_low = weights.astype(jnp.bfloat16)
        head_out = (jnp.dot(weights_low, v_head, preferred_element_type=jnp.float32) / totals).astype(jnp.bfloat16)
        return lax.dynamic_update_slice_in_dim(result, head_out, column, 1)
    start_value = jnp.zeros(query_block.shape, jnp.bfloat16)
    return lax.fori_loop(0, head_count, one_head, start_value)

def layer_norm(features, norm_gain, norm_bias):
    values_wide = features.astype(jnp.float32)
    center = lax.optimization_barrier(jnp.mean(values_wide, axis=1, keepdims=True))
    spread = lax.optimization_barrier(jnp.mean(jnp.square(values_wide - center), axis=1, keepdims=True))
    return ((values_wide - center) * lax.rsqrt(spread + 1e-06) * norm_gain + norm_bias).astype(jnp.bfloat16)

def reference(queries, keys, values, img_height, img_width, norm_gain, norm_bias):
    model_width = queries.shape[1]
    lengths = (img_height * img_width).astype(jnp.int32)
    image_ends = jnp.cumsum(lengths).astype(jnp.int32)
    token_ids = image_index(image_ends, jnp.arange(TOKENS, dtype=jnp.int32))
    margin = REACH * TOK_DEV
    zero_rows = jnp.zeros((margin, model_width), keys.dtype)
    keys_padded = jnp.concatenate([zero_rows, keys, zero_rows], axis=0)
    values_padded = jnp.concatenate([zero_rows, values, zero_rows], axis=0)
    missing = jnp.full((margin,), -1, jnp.int32)
    ids_padded = jnp.concatenate([missing, token_ids, missing], axis=0)
    window_rows = (2 * REACH + 1) * TOK_DEV

    def block_attention(block_index):
        start = (block_index * TOK_DEV).astype(jnp.int32)
        query_block = lax.dynamic_slice_in_dim(queries, start, TOK_DEV, 0)
        query_ids = lax.dynamic_slice_in_dim(token_ids, start, TOK_DEV, 0)
        key_window = lax.dynamic_slice_in_dim(keys_padded, start, window_rows, 0)
        value_window = lax.dynamic_slice_in_dim(values_padded, start, window_rows, 0)
        window_ids = lax.dynamic_slice_in_dim(ids_padded, start, window_rows, 0)
        allowed = query_ids[:, None] == window_ids[None, :]
        return head_attention(query_block, key_window, value_window, allowed)
    blocks = lax.map(block_attention, jnp.arange(TOKENS // TOK_DEV, dtype=jnp.int32))
    attention = blocks.reshape(TOKENS, model_width)
    targets = jnp.arange(MERGED, dtype=jnp.int32)
    owners = image_index(image_ends // 4, targets)
    starts = (image_ends - lengths).astype(jnp.int32)
    first = starts[owners]
    across = img_width[owners].astype(jnp.int32)
    within = targets - first // 4
    half_width = across // 2
    grid_row = within // half_width
    grid_col = within - grid_row * half_width
    source = (first + 2 * grid_row * across + 2 * grid_col).astype(jnp.int32)
    gathered = jnp.concatenate([attention[source], attention[source + 1], attention[source + across], attention[source + across + 1]], axis=1)
    return layer_norm(gathered, norm_gain, norm_bias)
```

```python
import functools
import math

import jax
import jax.numpy as jnp
from jax import lax
from jax.experimental import pallas as pl
from jax.experimental.pallas import tpu as pltpu
from jax.sharding import PartitionSpec as P

HEAD = 128
MOST = 896
WMAX = 32
GROUP = 8
ROWS = 256
HEADS = 3
WIDE = HEADS * HEAD
EXTRA = GROUP * WIDE
FULL = WIDE + HEAD
SPAN = GROUP * ROWS
KROWS = SPAN + 2 * MOST
QROWS = SPAN + 2 * WMAX
CHUNK = 256
CHUNKS = 10
QUERY_WINDOW = ROWS + 2 * WMAX
MESH = pl.DeviceIdType.MESH
NEG = -1e30
EXP_SCALE = math.log2(math.e) / math.sqrt(HEAD)


def remote(src, dst, send, recv, device):
    return pltpu.make_async_remote_copy(
        src_ref=src,
        dst_ref=dst,
        send_sem=send,
        recv_sem=recv,
        device_id=(device,),
        device_id_type=MESH,
    )


def greet(devices):
    barrier = pltpu.get_barrier_semaphore()
    for device in devices:
        pl.semaphore_signal(barrier, inc=1, device_id=(device,), device_id_type=MESH)
    pl.semaphore_wait(barrier, len(devices))


def head_columns(index):
    return pl.ds(pl.multiple_of(index * WIDE, HEAD), WIDE)


ORDER = (4, 3, 5, 2, 6, 1, 7)
MAIN = pl.ds(0, WIDE)
LAST = pl.ds(WIDE, HEAD)


def spread_kernel(
    count, k_in, v_in, q_in, k_out, v_out, q_out, stage,
    send, recv, send_last, recv_last, load_sem, store_sem,
    halo_send, halo_recv, halo_send_last, halo_recv_last,
):
    me = lax.axis_index("seq")
    j = lax.rem(me, GROUP)
    first = me - j
    above = lax.rem(me + GROUP, count)
    below = lax.rem(me + count - GROUP, count)
    greet([first + lax.rem(j + o, GROUP) for o in ORDER] + [above, below])
    tensors = ((k_in, k_out, MOST), (v_in, v_out, MOST), (q_in, q_out, WMAX))

    def own_rows(base):
        return pl.ds(pl.multiple_of(base + j * ROWS, 32), ROWS)

    def piece(t, o):
        source, target, base = tensors[t]
        to = lax.rem(j + o, GROUP)
        return remote(
            source.at[:, head_columns(to)], target.at[own_rows(base), MAIN],
            send.at[t, o], recv.at[t, j], first + to,
        )

    def piece_last(t):
        source, target, base = tensors[t]
        return remote(
            source.at[:, pl.ds(EXTRA, HEAD)], target.at[own_rows(base), LAST],
            send_last.at[t], recv_last.at[t, j], first + GROUP - 1,
        )

    def load(t):
        return pltpu.make_async_copy(
            tensors[t][0].at[:, head_columns(j)], stage.at[t, :, MAIN], load_sem.at[t, 0]
        )

    def load_last(t):
        return pltpu.make_async_copy(
            tensors[t][0].at[:, pl.ds(EXTRA, HEAD)], stage.at[t, :, LAST], load_sem.at[t, 1]
        )

    def store(t):
        return pltpu.make_async_copy(
            stage.at[t], tensors[t][1].at[own_rows(tensors[t][2]), :], store_sem.at[t]
        )

    for t in range(3):
        for o in ORDER:
            piece(t, o).start()

        @pl.when(j != GROUP - 1)
        def _():
            piece_last(t).start()

        load(t).start()
        load_last(t).start()
    for t in range(3):
        load(t).wait()
        load_last(t).wait()
        store(t).start()
    for t in range(3):
        store(t).wait()

    def arrival(t, s):
        source, target, base = tensors[t]
        rows = pl.ds(base + s * ROWS, ROWS)

        @pl.when(j != s)
        def _():
            remote(
                source.at[:, MAIN], target.at[rows, MAIN], send.at[t, 0], recv.at[t, s], me
            ).wait_recv()

            @pl.when(j == GROUP - 1)
            def _():
                remote(
                    source.at[:, pl.ds(EXTRA, HEAD)], target.at[rows, LAST],
                    send_last.at[t], recv_last.at[t, s], me,
                ).wait_recv()

    def halo(t, s):
        target, base = tensors[t][1:]
        size = SPAN + base
        if s < GROUP // 2:
            start, stop = s * ROWS, min((s + 1) * ROWS, base)
            device, origin, landing = below, base + start, size + start
        else:
            start, stop = max(s * ROWS, SPAN - base), (s + 1) * ROWS
            device, origin, landing = above, base + start, start - (SPAN - base)
        if stop <= start:
            return None
        length = stop - start

        def copy(columns, sends, recvs):
            return remote(
                target.at[pl.ds(origin, length), columns],
                target.at[pl.ds(landing, length), columns],
                sends.at[t, s], recvs.at[t, s], device,
            )

        return copy(MAIN, halo_send, halo_recv), copy(LAST, halo_send_last, halo_recv_last)

    copies = []
    for t in range(3):
        for s in (3, 4, 2, 5, 1, 6, 0, 7):
            arrival(t, s)
            both = halo(t, s)
            if both is not None:
                main, last = both
                main.start()

                @pl.when(j == GROUP - 1)
                def _():
                    last.start()

                copies.append(both)
    for main, last in copies:
        main.wait()

        @pl.when(j == GROUP - 1)
        def _():
            last.wait()

    for t in range(3):
        for o in ORDER:
            piece(t, o).wait_send()

        @pl.when(j != GROUP - 1)
        def _():
            piece_last(t).wait_send()


def spread(keys, values, queries, count):
    shape = jax.ShapeDtypeStruct
    dma = pltpu.SemaphoreType.DMA
    anywhere = pl.BlockSpec(memory_space=pl.ANY)
    return pl.pallas_call(
        functools.partial(spread_kernel, count),
        out_shape=(
            shape((KROWS, FULL), jnp.bfloat16),
            shape((KROWS, FULL), jnp.bfloat16),
            shape((QROWS, FULL), jnp.bfloat16),
        ),
        in_specs=[anywhere] * 3,
        out_specs=(anywhere,) * 3,
        scratch_shapes=[
            pltpu.VMEM((3, ROWS, FULL), jnp.bfloat16),
            dma((3, GROUP)), dma((3, GROUP)), dma((3,)), dma((3, GROUP)),
            dma((3, 2)), dma((3,)),
            dma((3, GROUP)), dma((3, GROUP)), dma((3, GROUP)), dma((3, GROUP)),
        ],
        compiler_params=pltpu.CompilerParams(collective_id=0, has_side_effects=True),
        name="spread",
    )(keys, values, queries)


def collect_kernel(o_in, a_out, stage, send, recv, send_last, recv_last, load_sem, store_sem):
    me = lax.axis_index("seq")
    j = lax.rem(me, GROUP)
    first = me - j
    greet([first + lax.rem(j + o, GROUP) for o in ORDER])

    def rows_of(index):
        return pl.ds(pl.multiple_of(index * ROWS, ROWS), ROWS)

    def piece(o):
        to = lax.rem(j + o, GROUP)
        return remote(
            o_in.at[rows_of(to), MAIN], a_out.at[:, head_columns(j)],
            send.at[o], recv.at[j], first + to,
        )

    def piece_last(o):
        to = lax.rem(j + o, GROUP)
        return remote(
            o_in.at[rows_of(to), LAST], a_out.at[:, pl.ds(EXTRA, HEAD)],
            send_last.at[o], recv_last, first + to,
        )

    load = pltpu.make_async_copy(o_in.at[rows_of(j), :], stage, load_sem)
    store = pltpu.make_async_copy(stage.at[:, MAIN], a_out.at[:, head_columns(j)], store_sem.at[0])
    store_last = pltpu.make_async_copy(
        stage.at[:, LAST], a_out.at[:, pl.ds(EXTRA, HEAD)], store_sem.at[1]
    )
    holder = j == GROUP - 1
    for o in ORDER:
        piece(o).start()

    @pl.when(holder)
    def _():
        for o in ORDER:
            piece_last(o).start()

    load.start()
    load.wait()
    store.start()

    @pl.when(holder)
    def _():
        store_last.start()
        store_last.wait()

    store.wait()
    for s in range(GROUP):

        @pl.when(j != s)
        def _():
            remote(
                o_in.at[pl.ds(0, ROWS), MAIN], a_out.at[:, pl.ds(s * WIDE, WIDE)],
                send.at[0], recv.at[s], me,
            ).wait_recv()

    @pl.when(jnp.logical_not(holder))
    def _():
        remote(
            o_in.at[pl.ds(0, ROWS), LAST], a_out.at[:, pl.ds(EXTRA, HEAD)],
            send_last.at[0], recv_last, me,
        ).wait_recv()

    for o in ORDER:
        piece(o).wait_send()

    @pl.when(holder)
    def _():
        for o in ORDER:
            piece_last(o).wait_send()


def collect(outputs, width):
    dma = pltpu.SemaphoreType.DMA
    anywhere = pl.BlockSpec(memory_space=pl.ANY)
    return pl.pallas_call(
        collect_kernel,
        out_shape=jax.ShapeDtypeStruct((ROWS, width), jnp.bfloat16),
        in_specs=[anywhere],
        out_specs=anywhere,
        scratch_shapes=[
            pltpu.VMEM((ROWS, FULL), jnp.bfloat16),
            dma((GROUP,)), dma((GROUP,)), dma((GROUP,)), dma(()), dma(()), dma((2,)),
        ],
        compiler_params=pltpu.CompilerParams(collective_id=1, has_side_effects=True),
        name="collect",
    )(outputs)


def attend_kernel(
    bounds, where, slots, k_ref, v_ref, q_ref, o_ref,
    query, scores, tops, sums, result,
):
    block = pl.program_id(0)
    merged = ROWS // 4
    row_index = where[0]
    targets = (
        row_index * (SPAN // 4) + block * merged
        + lax.broadcasted_iota(jnp.int32, (merged, 1), 0)
    )
    ends = slots[0:1, :]
    packed = slots[1:2, :]
    past = ends <= 4 * targets
    begin = jnp.max(jnp.where(past, ends, 0), axis=1, keepdims=True)
    found = jnp.min(jnp.where(past, 1 << 30, packed), axis=1, keepdims=True)
    finish = found // 64
    across = 32 - (found - finish * 64)
    half = across // 2
    within = targets - begin // 4
    grid_row = within // half
    grid_col = within - grid_row * half
    source = begin + 2 * grid_row * across + 2 * grid_col
    local = source - (row_index * SPAN - WMAX + block * ROWS)
    picks = jnp.concatenate([local, local + 1, local + across, local + across + 1], axis=0)
    lanes = lax.broadcasted_iota(jnp.int32, (ROWS, QUERY_WINDOW), 1)
    choose = jnp.where(lanes == picks, 1.0, 0.0).astype(jnp.bfloat16)
    window = q_ref[pl.ds(pl.multiple_of(block * ROWS, ROWS), QUERY_WINDOW), :]
    query[...] = jnp.dot(choose, window, preferred_element_type=jnp.float32).astype(jnp.bfloat16)
    offset = row_index * SPAN - MOST
    low_once = begin - offset
    high_once = finish - offset
    low = jnp.concatenate([low_once] * 4, axis=0)
    high = jnp.concatenate([high_once] * 4, axis=0)
    chunk_first = bounds[0, block] // CHUNK
    chunk_stop = (bounds[1, block] + CHUNK - 1) // CHUNK

    def run(heads):
        for h in heads:
            tops[h] = jnp.full((ROWS, HEAD), NEG, jnp.float32)
            sums[h] = jnp.zeros((ROWS, HEAD), jnp.float32)
            result[h] = jnp.zeros((ROWS, HEAD), jnp.float32)

        @pl.loop(chunk_first, chunk_stop)
        def _(c):
            rows = pl.ds(pl.multiple_of(c * CHUNK, CHUNK), CHUNK)
            places = c * CHUNK + lax.broadcasted_iota(jnp.int32, (1, CHUNK), 1)
            kept = (places >= low) & (places < high)
            for h in heads:
                columns = pl.ds(h * HEAD, HEAD)
                part = lax.dot_general(
                    query[:, columns], k_ref[rows, columns], (((1,), (1,)), ((), ())),
                    preferred_element_type=jnp.float32,
                )
                part = jnp.where(kept, part, NEG)
                scores[h, c - chunk_first] = part
                best = tops[h]
                for g in range(CHUNK // HEAD):
                    best = jnp.maximum(best, part[:, g * HEAD:(g + 1) * HEAD])
                tops[h] = best

        for h in heads:
            tops[h] = jnp.broadcast_to(
                jnp.max(tops[h], axis=1, keepdims=True), (ROWS, HEAD)
            )

        @pl.loop(chunk_first, chunk_stop)
        def _(c):
            rows = pl.ds(pl.multiple_of(c * CHUNK, CHUNK), CHUNK)
            for h in heads:
                columns = pl.ds(h * HEAD, HEAD)
                top = jnp.concatenate([tops[h]] * (CHUNK // HEAD), axis=1)
                weights = jnp.exp2((scores[h, c - chunk_first] - top) * EXP_SCALE)
                total = sums[h]
                for g in range(CHUNK // HEAD):
                    total = total + weights[:, g * HEAD:(g + 1) * HEAD]
                sums[h] = total
                result[h] += jnp.dot(
                    weights.astype(jnp.bfloat16), v_ref[rows, columns],
                    preferred_element_type=jnp.float32,
                )

        for h in heads:
            total = jnp.sum(sums[h], axis=1, keepdims=True)
            o_ref[:, pl.ds(h * HEAD, HEAD)] = (result[h] / total).astype(jnp.bfloat16)

    @pl.when(where[1] == GROUP - 1)
    def _():
        run((0, 1, 2, 3))

    @pl.when(where[1] != GROUP - 1)
    def _():
        run((0, 1, 2))


def attend(bounds, where, slots, keys, values, queries):
    whole = lambda shape: pl.BlockSpec(shape, lambda i, *_: (0, 0), pipeline_mode=pl.Buffered(1))
    return pl.pallas_call(
        attend_kernel,
        out_shape=jax.ShapeDtypeStruct((SPAN, FULL), jnp.bfloat16),
        grid_spec=pltpu.PrefetchScalarGridSpec(
            num_scalar_prefetch=2,
            grid=(GROUP,),
            in_specs=[
                whole(slots.shape), whole(keys.shape), whole(values.shape), whole(queries.shape)
            ],
            out_specs=pl.BlockSpec((ROWS, FULL), lambda i, *_: (i, 0)),
            scratch_shapes=[
                pltpu.VMEM((ROWS, FULL), jnp.bfloat16),
                pltpu.VMEM((4, CHUNKS, ROWS, CHUNK), jnp.float32),
                pltpu.VMEM((4, ROWS, HEAD), jnp.float32),
                pltpu.VMEM((4, ROWS, HEAD), jnp.float32),
                pltpu.VMEM((4, ROWS, HEAD), jnp.float32),
            ],
        ),
        name="attend",
    )(bounds, where, slots, keys, values, queries)


def norm_kernel(width, a_ref, gain_ref, bias_ref, o_ref):
    parts = [a_ref[g].astype(jnp.float32) for g in range(4)]
    features = 4 * width
    center = sum(jnp.sum(p, axis=1, keepdims=True) for p in parts) / features
    spread_sum = sum(jnp.sum(jnp.square(p - center), axis=1, keepdims=True) for p in parts)
    scale = lax.rsqrt(spread_sum / features + 1e-06)
    for g in range(4):
        columns = pl.ds(g * width, width)
        o_ref[:, columns] = (
            (parts[g] - center) * scale * gain_ref[:, columns] + bias_ref[:, columns]
        ).astype(jnp.bfloat16)


def norm(attention, gain, bias):
    rows, width = attention.shape
    merged = rows // 4
    step = 16
    fixed = pl.BlockSpec((1, 4 * width), lambda i: (0, 0))
    return pl.pallas_call(
        functools.partial(norm_kernel, width),
        out_shape=jax.ShapeDtypeStruct((merged, 4 * width), jnp.bfloat16),
        grid=(merged // step,),
        in_specs=[pl.BlockSpec((4, step, width), lambda i: (0, i, 0)), fixed, fixed],
        out_specs=pl.BlockSpec((step, 4 * width), lambda i: (i, 0)),
        name="norm",
    )(attention.reshape(4, merged, width), gain.reshape(1, -1), bias.reshape(1, -1))


def body(queries, keys, values, img_height, img_width, norm_gain, norm_bias):
    count = lax.axis_size("seq")
    device = lax.axis_index("seq")
    row_index = device // GROUP
    ends = jnp.cumsum(img_height * img_width)
    packed = ends * 64 + (32 - img_width)
    slot_count = ends.shape[0]
    pad = -slot_count % 128
    last = jnp.full((pad,), 1 << 30, jnp.int32)
    slots = jnp.stack([jnp.concatenate([ends, last]), jnp.concatenate([packed, last])])
    firsts = 4 * (row_index * (SPAN // 4) + jnp.arange(GROUP, dtype=jnp.int32) * (ROWS // 4))
    lows = jnp.max(jnp.where(ends[None, :] <= firsts[:, None], ends[None, :], 0), axis=1)
    finals = firsts + ROWS - 4
    highs = jnp.min(jnp.where(ends[None, :] > finals[:, None], ends[None, :], 1 << 30), axis=1)
    bounds = jnp.stack([lows, highs]) - (row_index * SPAN - MOST)
    where = jnp.stack([row_index, device % GROUP])
    k_row, v_row, q_row = spread(keys, values, queries, count)
    outputs = attend(bounds, where, slots, k_row, v_row, q_row)
    return norm(collect(outputs, queries.shape[1]), norm_gain, norm_bias)


def solution(mesh):
    in_specs = (P("seq", None), P("seq", None), P("seq", None), P(), P(), P(), P())
    out_specs = P("seq", None)
    return jax.shard_map(body, mesh=mesh, in_specs=in_specs, out_specs=out_specs, check_vma=False)
```

```python
import functools
import math

import jax
import jax.numpy as jnp
from jax import lax
from jax.experimental import pallas as pl
from jax.experimental.pallas import tpu as pltpu
from jax.sharding import PartitionSpec as P

HEAD = 128
MOST = 896
WMAX = 32
GROUP = 8
ROWS = 256
HEADS = 3
ALL_HEADS = GROUP * HEADS + 1
MERGED = ROWS // 4
SPAN = GROUP * ROWS
KROWS = SPAN + 2 * MOST
QROWS = SPAN + 2 * WMAX
WINDOW = 2048
CHUNK = 512
QUERY_WINDOW = ROWS + 2 * WMAX
MESH = pl.DeviceIdType.MESH
NEG = -1e30
EXP_SCALE = math.log2(math.e) / math.sqrt(HEAD)
ORDER = (4, 3, 5, 2, 6, 1, 7)
SOURCES = (3, 4, 2, 5, 1, 6, 0, 7)


def remote(src, dst, send, recv, device):
    return pltpu.make_async_remote_copy(
        src_ref=src,
        dst_ref=dst,
        send_sem=send,
        recv_sem=recv,
        device_id=(device,),
        device_id_type=MESH,
    )


def greet(devices):
    barrier = pltpu.get_barrier_semaphore()
    for device in devices:
        pl.semaphore_signal(barrier, inc=1, device_id=(device,), device_id_type=MESH)
    pl.semaphore_wait(barrier, len(devices))


def spread_lanes(column):
    return jnp.broadcast_to(column, (column.shape[0], HEAD))


def four(column):
    return jnp.concatenate([column] * 4, axis=0)


def plan_blocks(row_index, slots, picks_ref, mask_ref):
    slot_rows = slots.shape[1]

    @pl.loop(0, GROUP)
    def _(i):
        targets = (
            row_index * (SPAN // 4) + i * MERGED
            + lax.broadcasted_iota(jnp.int32, (MERGED, HEAD), 0)
        )
        begin = jnp.zeros((MERGED, HEAD), jnp.int32)
        found = jnp.full((MERGED, HEAD), 1 << 30, jnp.int32)
        for r in range(slot_rows):
            ends = slots[0, r:r + 1, :]
            past = ends <= 4 * targets
            begin = jnp.maximum(begin, jnp.where(past, ends, 0))
            found = jnp.minimum(found, jnp.where(past, 1 << 30, slots[1, r:r + 1, :]))
        begin = spread_lanes(jnp.max(begin, axis=1, keepdims=True))
        found = spread_lanes(jnp.min(found, axis=1, keepdims=True))
        finish = lax.shift_right_logical(found, 6)
        across = 32 - (found & 63)
        half = lax.shift_right_logical(across, 1)
        within = targets - lax.shift_right_logical(begin, 2)
        grid_row = (
            (within.astype(jnp.float32) + 0.5) / half.astype(jnp.float32)
        ).astype(jnp.int32)
        grid_col = within - grid_row * half
        source = begin + 2 * grid_row * across + 2 * grid_col
        local = source - (row_index * SPAN - WMAX + i * ROWS)
        rows = pl.ds(pl.multiple_of(i * ROWS, ROWS), ROWS)
        picks_ref[rows, :] = jnp.concatenate(
            [local, local + 1, local + across, local + across + 1], axis=0
        )
        offset = row_index * SPAN - MOST + i * ROWS
        low, high = begin - offset, finish - offset
        lane = lax.broadcasted_iota(jnp.int32, (MERGED, HEAD), 1)
        for g in range(WINDOW // HEAD):
            place = lane + g * HEAD
            kept = jnp.where((place >= low) & (place < high), 0.0, NEG)
            mask_ref[rows, pl.ds(g * HEAD, HEAD)] = four(kept)


def attend_block(i, q_buf, k_buf, v_buf, picks_ref, mask_ref, scores):
    base = pl.multiple_of(i * ROWS, ROWS)
    rows = pl.ds(base, ROWS)
    picks = picks_ref[rows, :]
    lane = lax.broadcasted_iota(jnp.int32, (ROWS, HEAD), 1)
    choose = jnp.concatenate(
        [jnp.where(lane + g * HEAD == picks, 1.0, 0.0) for g in range(3)], axis=1
    )[:, :QUERY_WINDOW].astype(jnp.bfloat16)
    query = jnp.dot(
        choose, q_buf[pl.ds(base, QUERY_WINDOW), :], preferred_element_type=jnp.float32
    ).astype(jnp.bfloat16)
    best = jnp.full((ROWS, HEAD), NEG, jnp.float32)
    for c in range(WINDOW // CHUNK):
        part = lax.dot_general(
            query, k_buf[pl.ds(base + c * CHUNK, CHUNK), :], (((1,), (1,)), ((), ())),
            preferred_element_type=jnp.float32,
        ) + mask_ref[rows, pl.ds(c * CHUNK, CHUNK)]
        scores[:, pl.ds(c * CHUNK, CHUNK)] = part
        for g in range(CHUNK // HEAD):
            best = jnp.maximum(best, part[:, g * HEAD:(g + 1) * HEAD])
    top = spread_lanes(jnp.max(best, axis=1, keepdims=True))
    tops = jnp.concatenate([top] * (CHUNK // HEAD), axis=1)
    total = jnp.zeros((ROWS, HEAD), jnp.float32)
    result = jnp.zeros((ROWS, HEAD), jnp.float32)
    for c in range(WINDOW // CHUNK):
        weights = jnp.exp2((scores[:, pl.ds(c * CHUNK, CHUNK)] - tops) * EXP_SCALE)
        for g in range(CHUNK // HEAD):
            total = total + weights[:, g * HEAD:(g + 1) * HEAD]
        result = result + jnp.dot(
            weights.astype(jnp.bfloat16), v_buf[pl.ds(base + c * CHUNK, CHUNK), :],
            preferred_element_type=jnp.float32,
        )
    return (result / jnp.sum(total, axis=1, keepdims=True)).astype(jnp.bfloat16)


def normalize(landed, gain_ref, bias_ref, out_ref):
    step = 16
    features = 4 * ALL_HEADS * HEAD

    @pl.loop(0, MERGED // step)
    def _(g):
        first = pl.multiple_of(g * step, step)

        def tile(quarter, head):
            start = pl.multiple_of(quarter * MERGED + first, step)
            return landed[head, pl.ds(start, step), :].astype(jnp.float32)

        places = [(q, h) for q in range(4) for h in range(ALL_HEADS)]
        total = sum(tile(*place) for place in places)
        center = spread_lanes(jnp.sum(total, axis=1, keepdims=True) / features)
        squares = sum(jnp.square(tile(*place) - center) for place in places)
        scale = spread_lanes(
            lax.rsqrt(jnp.sum(squares, axis=1, keepdims=True) / features + 1e-06)
        )
        for index, place in enumerate(places):
            out_ref[pl.ds(first, step), pl.ds(index * HEAD, HEAD)] = (
                (tile(*place) - center) * scale * gain_ref[index:index + 1, :]
                + bias_ref[index:index + 1, :]
            ).astype(jnp.bfloat16)


def kernel(
    count, slots, k_in, v_in, q_in, gain_ref, bias_ref, out_ref,
    k_buf, v_buf, q_buf, outs, landed, picks_ref, mask_ref, scores,
    send, recv, load_sem, halo_send, halo_recv, out_send, out_recv,
):
    me = lax.axis_index("seq")
    j = lax.rem(me, GROUP)
    first = me - j
    row_index = me // GROUP
    above = lax.rem(me + GROUP, count)
    below = lax.rem(me + count - GROUP, count)
    holder = j == GROUP - 1
    greet([first + lax.rem(j + o, GROUP) for o in ORDER] + [above, below])
    tensors = ((k_in, k_buf, MOST), (v_in, v_buf, MOST), (q_in, q_buf, WMAX))

    def columns_of(index, n):
        head = GROUP * HEADS if n == HEADS else index * HEADS + n
        return pl.ds(pl.multiple_of(head * HEAD, HEAD), HEAD)

    def own_rows(base):
        return pl.ds(pl.multiple_of(base + j * ROWS, 32), ROWS)

    def piece(n, t, o):
        source, target, base = tensors[t]
        to = GROUP - 1 if n == HEADS else lax.rem(j + o, GROUP)
        return remote(
            source.at[:, columns_of(to, n)], target.at[n, own_rows(base), :],
            send.at[n, t, o], recv.at[n, t, j], first + to,
        )

    def own(n, t):
        source, target, base = tensors[t]
        return pltpu.make_async_copy(
            source.at[:, columns_of(j, n)], target.at[n, own_rows(base), :], load_sem.at[n, t]
        )

    def each_piece(n, act):
        for t in range(3):
            if n == HEADS:

                @pl.when(jnp.logical_not(holder))
                def _():
                    act(piece(n, t, 0))

            else:
                for o in ORDER:
                    act(piece(n, t, o))

    def start_stage(n):
        each_piece(n, lambda copy: copy.start())
        for t in range(3):
            if n == HEADS:

                @pl.when(holder)
                def _():
                    own(n, t).start()

            else:
                own(n, t).start()

    def halo(n, t, s):
        target, base = tensors[t][1:]
        if s < GROUP // 2:
            start, stop = s * ROWS, min((s + 1) * ROWS, base)
            device, landing = below, base + SPAN + start
        else:
            start, stop = max(s * ROWS, SPAN - base), (s + 1) * ROWS
            device, landing = above, start - (SPAN - base)
        if stop <= start:
            return None
        return remote(
            target.at[n, pl.ds(base + start, stop - start), :],
            target.at[n, pl.ds(landing, stop - start), :],
            halo_send.at[n, t, s], halo_recv.at[n, t, s], device,
        )

    def arrive(n):
        for t in range(3):
            for s in SOURCES:
                source, target, base = tensors[t]

                @pl.when(j != s)
                def _():
                    remote(
                        source.at[:, pl.ds(0, HEAD)],
                        target.at[n, pl.ds(base + s * ROWS, ROWS), :],
                        send.at[n, t, 0], recv.at[n, t, s], me,
                    ).wait_recv()

                @pl.when(j == s)
                def _():
                    own(n, t).wait()

                copy = halo(n, t, s)
                if copy is not None:
                    copy.start()
        for t in range(3):
            for s in SOURCES:
                copy = halo(n, t, s)
                if copy is not None:
                    copy.wait_recv()

    def output(n, i):
        head = GROUP * HEADS if n == HEADS else j * HEADS + n
        rows = pl.ds(pl.multiple_of(i * ROWS, ROWS), ROWS)
        return remote(
            outs.at[n, rows, :], landed.at[head], out_send.at[n, i], out_recv.at[n, j], first + i
        )

    def compute(n):
        head = GROUP * HEADS if n == HEADS else j * HEADS + n

        @pl.loop(0, GROUP)
        def _(i):
            block = attend_block(
                i, q_buf.at[n], k_buf.at[n], v_buf.at[n], picks_ref, mask_ref, scores
            )
            outs[n, pl.ds(pl.multiple_of(i * ROWS, ROWS), ROWS), :] = block

            @pl.when(i == j)
            def _():
                landed[head] = block

            @pl.when((i > 0) & (i - 1 != j))
            def _():
                output(n, i - 1).start()

        @pl.when(jnp.logical_not(holder))
        def _():
            output(n, GROUP - 1).start()

    start_stage(0)
    start_stage(1)
    plan_blocks(row_index, slots, picks_ref, mask_ref)
    arrive(0)
    start_stage(3)
    start_stage(2)
    compute(0)
    arrive(1)
    compute(1)

    @pl.when(holder)
    def _():
        arrive(3)
        compute(3)

    arrive(2)
    compute(2)

    for n in range(HEADS):
        for s in range(GROUP):

            @pl.when(j != s)
            def _():
                remote(
                    outs.at[n, pl.ds(0, ROWS), :], landed.at[s * HEADS + n],
                    out_send.at[n, 0], out_recv.at[n, s], me,
                ).wait_recv()

    @pl.when(jnp.logical_not(holder))
    def _():
        remote(
            outs.at[HEADS, pl.ds(0, ROWS), :], landed.at[GROUP * HEADS],
            out_send.at[HEADS, 0], out_recv.at[HEADS, GROUP - 1], me,
        ).wait_recv()

    normalize(landed, gain_ref, bias_ref, out_ref)

    def finish(n):
        for t in range(3):
            for s in SOURCES:
                copy = halo(n, t, s)
                if copy is not None:
                    copy.wait_send()
        for i in range(GROUP):

            @pl.when(j != i)
            def _():
                output(n, i).wait_send()

    for n in range(HEADS + 1):
        each_piece(n, lambda copy: copy.wait_send())
        if n == HEADS:
            pl.when(holder)(functools.partial(finish, n))
        else:
            finish(n)


def body(queries, keys, values, img_height, img_width, norm_gain, norm_bias):
    count = lax.axis_size("seq")
    features = norm_gain.shape[0]
    ends = jnp.cumsum(img_height * img_width)
    packed = ends * 64 + (32 - img_width)
    pad = -ends.shape[0] % HEAD
    slots = jnp.pad(
        jnp.stack([ends, packed]), ((0, 0), (0, pad)), constant_values=1 << 30
    ).reshape(2, -1, HEAD)
    dma = pltpu.SemaphoreType.DMA
    anywhere = pl.BlockSpec(memory_space=pl.ANY)
    resident = pl.BlockSpec(memory_space=pltpu.VMEM)
    stages = HEADS + 1
    return pl.pallas_call(
        functools.partial(kernel, count),
        out_shape=jax.ShapeDtypeStruct((MERGED, features), jnp.bfloat16),
        in_specs=[resident, anywhere, anywhere, anywhere, resident, resident],
        out_specs=resident,
        scratch_shapes=[
            pltpu.VMEM((stages, KROWS, HEAD), jnp.bfloat16),
            pltpu.VMEM((stages, KROWS, HEAD), jnp.bfloat16),
            pltpu.VMEM((stages, QROWS, HEAD), jnp.bfloat16),
            pltpu.VMEM((stages, SPAN, HEAD), jnp.bfloat16),
            pltpu.VMEM((ALL_HEADS, ROWS, HEAD), jnp.bfloat16),
            pltpu.VMEM((SPAN, HEAD), jnp.int32),
            pltpu.VMEM((SPAN, WINDOW), jnp.float32),
            pltpu.VMEM((ROWS, WINDOW), jnp.float32),
            dma((stages, 3, GROUP)), dma((stages, 3, GROUP)), dma((stages, 3)),
            dma((stages, 3, GROUP)), dma((stages, 3, GROUP)),
            dma((stages, GROUP)), dma((stages, GROUP)),
        ],
        compiler_params=pltpu.CompilerParams(
            collective_id=0, has_side_effects=True, vmem_limit_bytes=60 * 1024 * 1024
        ),
        name="packed_attention",
    )(
        slots, keys, values, queries,
        norm_gain.reshape(-1, HEAD), norm_bias.reshape(-1, HEAD),
    )


def solution(mesh):
    in_specs = (P("seq", None), P("seq", None), P("seq", None), P(), P(), P(), P())
    out_specs = P("seq", None)
    return jax.shard_map(body, mesh=mesh, in_specs=in_specs, out_specs=out_specs, check_vma=False)
```

```python
import functools
import math

import jax
import jax.numpy as jnp
from jax import lax
from jax.experimental import pallas as pl
from jax.experimental.pallas import tpu as pltpu
from jax.sharding import PartitionSpec as P

HEAD = 128
MOST = 896
WMAX = 32
GROUP = 8
ROWS = 256
HEADS = 3
ALL_HEADS = GROUP * HEADS + 1
MERGED = ROWS // 4
SPAN = GROUP * ROWS
KROWS = SPAN + 2 * MOST
QROWS = SPAN + 2 * WMAX
WINDOW = 2048
CHUNK = 512
QUERY_WINDOW = ROWS + 2 * WMAX
MESH = pl.DeviceIdType.MESH
NEG = -1e30
EXP_SCALE = math.log2(math.e) / math.sqrt(HEAD)
ORDER = (4, 3, 5, 2, 6, 1, 7)
SOURCES = (3, 4, 2, 5, 1, 6, 0, 7)


def remote(src, dst, send, recv, device):
    return pltpu.make_async_remote_copy(
        src_ref=src,
        dst_ref=dst,
        send_sem=send,
        recv_sem=recv,
        device_id=(device,),
        device_id_type=MESH,
    )


def greet(devices):
    barrier = pltpu.get_barrier_semaphore()
    for device in devices:
        pl.semaphore_signal(barrier, inc=1, device_id=(device,), device_id_type=MESH)
    pl.semaphore_wait(barrier, len(devices))


def spread_lanes(column):
    return jnp.broadcast_to(column, (column.shape[0], HEAD))


def four(column):
    return jnp.concatenate([column] * 4, axis=0)


def plan_blocks(row_index, slots, picks_ref, mask_ref):
    slot_rows = slots.shape[1]

    @pl.loop(0, GROUP)
    def _(i):
        targets = (
            row_index * (SPAN // 4) + i * MERGED
            + lax.broadcasted_iota(jnp.int32, (MERGED, HEAD), 0)
        )
        begin = jnp.zeros((MERGED, HEAD), jnp.int32)
        found = jnp.full((MERGED, HEAD), 1 << 30, jnp.int32)
        for r in range(slot_rows):
            ends = slots[0, r:r + 1, :]
            past = ends <= 4 * targets
            begin = jnp.maximum(begin, jnp.where(past, ends, 0))
            found = jnp.minimum(found, jnp.where(past, 1 << 30, slots[1, r:r + 1, :]))
        begin = spread_lanes(jnp.max(begin, axis=1, keepdims=True))
        found = spread_lanes(jnp.min(found, axis=1, keepdims=True))
        finish = lax.shift_right_logical(found, 6)
        across = 32 - (found & 63)
        half = lax.shift_right_logical(across, 1)
        within = targets - lax.shift_right_logical(begin, 2)
        grid_row = (
            (within.astype(jnp.float32) + 0.5) / half.astype(jnp.float32)
        ).astype(jnp.int32)
        grid_col = within - grid_row * half
        source = begin + 2 * grid_row * across + 2 * grid_col
        local = source - (row_index * SPAN - WMAX + i * ROWS)
        rows = pl.ds(pl.multiple_of(i * ROWS, ROWS), ROWS)
        picks_ref[rows, :] = jnp.concatenate(
            [local, local + 1, local + across, local + across + 1], axis=0
        )
        offset = row_index * SPAN - MOST + i * ROWS
        low, high = begin - offset, finish - offset
        lane = lax.broadcasted_iota(jnp.int32, (MERGED, HEAD), 1)
        for g in range(WINDOW // HEAD):
            place = lane + g * HEAD
            kept = jnp.where((place >= low) & (place < high), 0.0, NEG)
            mask_ref[rows, pl.ds(g * HEAD, HEAD)] = four(kept)


def pick_queries(i, q_buf, picks_ref):
    base = pl.multiple_of(i * ROWS, ROWS)
    picks = picks_ref[pl.ds(base, ROWS), :]
    lane = lax.broadcasted_iota(jnp.int32, (ROWS, HEAD), 1)
    choose = jnp.concatenate(
        [jnp.where(lane + g * HEAD == picks, 1.0, 0.0) for g in range(3)], axis=1
    )[:, :QUERY_WINDOW].astype(jnp.bfloat16)
    return jnp.dot(
        choose, q_buf[pl.ds(base, QUERY_WINDOW), :], preferred_element_type=jnp.float32
    ).astype(jnp.bfloat16)


def score_chunk(query, i, c, best, k_buf, mask_ref, scores):
    base = pl.multiple_of(i * ROWS, ROWS)
    part = lax.dot_general(
        query, k_buf[pl.ds(base + c * CHUNK, CHUNK), :], (((1,), (1,)), ((), ())),
        preferred_element_type=jnp.float32,
    ) + mask_ref[pl.ds(base, ROWS), pl.ds(c * CHUNK, CHUNK)]
    scores[:, pl.ds(c * CHUNK, CHUNK)] = part
    for g in range(CHUNK // HEAD):
        best = jnp.maximum(best, part[:, g * HEAD:(g + 1) * HEAD])
    return best


def lowest():
    return jnp.full((ROWS, HEAD), NEG, jnp.float32)


def first_scores(q_buf, k_buf, picks_ref, mask_ref, scores, tops):
    query = pick_queries(0, q_buf, picks_ref)
    best = lowest()
    for c in range(WINDOW // CHUNK):
        best = score_chunk(query, 0, c, best, k_buf, mask_ref, scores)
    tops[...] = spread_lanes(jnp.max(best, axis=1, keepdims=True))


def attend_step(i, q_buf, k_buf, v_buf, picks_ref, mask_ref, now, later):
    scores, tops = now
    later_scores, later_tops = later
    base = pl.multiple_of(i * ROWS, ROWS)
    following = jnp.minimum(i + 1, GROUP - 1)
    query = pick_queries(following, q_buf, picks_ref)
    best = lowest()
    top = jnp.concatenate([tops[...]] * (CHUNK // HEAD), axis=1)
    total = jnp.zeros((ROWS, HEAD), jnp.float32)
    result = jnp.zeros((ROWS, HEAD), jnp.float32)
    for c in range(WINDOW // CHUNK):
        best = score_chunk(query, following, c, best, k_buf, mask_ref, later_scores)
        weights = jnp.exp2((scores[:, pl.ds(c * CHUNK, CHUNK)] - top) * EXP_SCALE)
        for g in range(CHUNK // HEAD):
            total = total + weights[:, g * HEAD:(g + 1) * HEAD]
        result = result + jnp.dot(
            weights.astype(jnp.bfloat16), v_buf[pl.ds(base + c * CHUNK, CHUNK), :],
            preferred_element_type=jnp.float32,
        )
    later_tops[...] = spread_lanes(jnp.max(best, axis=1, keepdims=True))
    return (result / jnp.sum(total, axis=1, keepdims=True)).astype(jnp.bfloat16)


def normalize(landed, gain_ref, bias_ref, out_ref):
    step = 16
    features = 4 * ALL_HEADS * HEAD

    @pl.loop(0, MERGED // step)
    def _(g):
        first = pl.multiple_of(g * step, step)

        def tile(quarter, head):
            start = pl.multiple_of(quarter * MERGED + first, step)
            return landed[head, pl.ds(start, step), :].astype(jnp.float32)

        places = [(q, h) for q in range(4) for h in range(ALL_HEADS)]
        total = sum(tile(*place) for place in places)
        center = spread_lanes(jnp.sum(total, axis=1, keepdims=True) / features)
        squares = sum(jnp.square(tile(*place) - center) for place in places)
        scale = spread_lanes(
            lax.rsqrt(jnp.sum(squares, axis=1, keepdims=True) / features + 1e-06)
        )
        for index, place in enumerate(places):
            out_ref[pl.ds(first, step), pl.ds(index * HEAD, HEAD)] = (
                (tile(*place) - center) * scale * gain_ref[index:index + 1, :]
                + bias_ref[index:index + 1, :]
            ).astype(jnp.bfloat16)


def kernel(
    count, slots, k_in, v_in, q_in, gain_ref, bias_ref, out_ref,
    k_buf, v_buf, q_buf, outs, landed, picks_ref, mask_ref,
    scores_a, scores_b, tops_a, tops_b,
    send, recv, load_sem, halo_send, halo_recv, out_send, out_recv,
):
    me = lax.axis_index("seq")
    j = lax.rem(me, GROUP)
    first = me - j
    row_index = me // GROUP
    above = lax.rem(me + GROUP, count)
    below = lax.rem(me + count - GROUP, count)
    holder = j == GROUP - 1
    greet([first + lax.rem(j + o, GROUP) for o in ORDER] + [above, below])
    tensors = ((k_in, k_buf, MOST), (v_in, v_buf, MOST), (q_in, q_buf, WMAX))

    def columns_of(index, n):
        head = GROUP * HEADS if n == HEADS else index * HEADS + n
        return pl.ds(pl.multiple_of(head * HEAD, HEAD), HEAD)

    def own_rows(base):
        return pl.ds(pl.multiple_of(base + j * ROWS, 32), ROWS)

    def piece(n, t, o):
        source, target, base = tensors[t]
        to = GROUP - 1 if n == HEADS else lax.rem(j + o, GROUP)
        return remote(
            source.at[:, columns_of(to, n)], target.at[n, own_rows(base), :],
            send.at[n, t, o], recv.at[n, t, j], first + to,
        )

    def own(n, t):
        source, target, base = tensors[t]
        return pltpu.make_async_copy(
            source.at[:, columns_of(j, n)], target.at[n, own_rows(base), :], load_sem.at[n, t]
        )

    def each_piece(n, act, only=(0, 1, 2)):
        for t in only:
            if n == HEADS:

                @pl.when(jnp.logical_not(holder))
                def _():
                    act(piece(n, t, 0))

            else:
                for o in ORDER:
                    act(piece(n, t, o))

    def depart(n, only=(0, 1, 2)):
        each_piece(n, lambda copy: copy.start(), only)
        for t in only:
            if n == HEADS:

                @pl.when(holder)
                def _():
                    own(n, t).start()

            else:
                own(n, t).start()

    def halo(n, t, s):
        target, base = tensors[t][1:]
        if s < GROUP // 2:
            start, stop = s * ROWS, min((s + 1) * ROWS, base)
            device, landing = below, base + SPAN + start
        else:
            start, stop = max(s * ROWS, SPAN - base), (s + 1) * ROWS
            device, landing = above, start - (SPAN - base)
        if stop <= start:
            return None
        return remote(
            target.at[n, pl.ds(base + start, stop - start), :],
            target.at[n, pl.ds(landing, stop - start), :],
            halo_send.at[n, t, s], halo_recv.at[n, t, s], device,
        )

    def arrive(n, only=(0, 1, 2)):
        for t in only:
            for s in SOURCES:
                source, target, base = tensors[t]

                @pl.when(j != s)
                def _():
                    remote(
                        source.at[:, pl.ds(0, HEAD)],
                        target.at[n, pl.ds(base + s * ROWS, ROWS), :],
                        send.at[n, t, 0], recv.at[n, t, s], me,
                    ).wait_recv()

                @pl.when(j == s)
                def _():
                    own(n, t).wait()

                copy = halo(n, t, s)
                if copy is not None:
                    copy.start()

    def complete(n):
        for t in range(3):
            for s in SOURCES:
                copy = halo(n, t, s)
                if copy is not None:
                    copy.wait_recv()

    def output(n, i):
        head = GROUP * HEADS if n == HEADS else j * HEADS + n
        rows = pl.ds(pl.multiple_of(i * ROWS, ROWS), ROWS)
        return remote(
            outs.at[n, rows, :], landed.at[head], out_send.at[n, i], out_recv.at[n, j], first + i
        )

    def compute(n, events=()):
        head = GROUP * HEADS if n == HEADS else j * HEADS + n

        first_scores(q_buf.at[n], k_buf.at[n], picks_ref, mask_ref, scores_a, tops_a)

        def block_step(i, now, later):
            block = attend_step(
                i, q_buf.at[n], k_buf.at[n], v_buf.at[n], picks_ref, mask_ref, now, later
            )
            outs[n, pl.ds(pl.multiple_of(i * ROWS, ROWS), ROWS), :] = block

            @pl.when(i == j)
            def _():
                landed[head] = block

            @pl.when((i > 0) & (i - 1 != j))
            def _():
                output(n, i - 1).start()

        @pl.loop(0, GROUP // 2)
        def _(pair):
            for turn, event in events:
                pl.when(pair == turn)(event)
            block_step(2 * pair, (scores_a, tops_a), (scores_b, tops_b))
            block_step(2 * pair + 1, (scores_b, tops_b), (scores_a, tops_a))

        @pl.when(jnp.logical_not(holder))
        def _():
            output(n, GROUP - 1).start()

    KEYS, VALUES, QUERIES = (0,), (1,), (2,)
    depart(0)
    plan_blocks(row_index, slots, picks_ref, mask_ref)
    arrive(0, KEYS)
    depart(1, KEYS)
    arrive(0, VALUES)
    depart(1, VALUES)
    arrive(0, QUERIES)
    depart(1, QUERIES)
    depart(3)
    complete(0)

    def during_first():
        arrive(1, KEYS)
        depart(2, KEYS)

    compute(0, [(2, during_first)])
    arrive(1, VALUES)
    depart(2, VALUES)
    arrive(1, QUERIES)
    depart(2, QUERIES)
    complete(1)

    def during_second():
        pl.when(holder)(lambda: arrive(3))

    compute(1, [(3, during_second)])

    @pl.when(holder)
    def _():
        complete(3)
        compute(3, [(0, lambda: arrive(2, KEYS)), (2, lambda: arrive(2, VALUES))])

    @pl.when(jnp.logical_not(holder))
    def _():
        arrive(2, KEYS)
        arrive(2, VALUES)

    arrive(2, QUERIES)
    complete(2)
    compute(2)

    for n in range(HEADS):
        for s in range(GROUP):

            @pl.when(j != s)
            def _():
                remote(
                    outs.at[n, pl.ds(0, ROWS), :], landed.at[s * HEADS + n],
                    out_send.at[n, 0], out_recv.at[n, s], me,
                ).wait_recv()

    @pl.when(jnp.logical_not(holder))
    def _():
        remote(
            outs.at[HEADS, pl.ds(0, ROWS), :], landed.at[GROUP * HEADS],
            out_send.at[HEADS, 0], out_recv.at[HEADS, GROUP - 1], me,
        ).wait_recv()

    normalize(landed, gain_ref, bias_ref, out_ref)

    def finish(n):
        for t in range(3):
            for s in SOURCES:
                copy = halo(n, t, s)
                if copy is not None:
                    copy.wait_send()
        for i in range(GROUP):

            @pl.when(j != i)
            def _():
                output(n, i).wait_send()

    for n in range(HEADS + 1):
        each_piece(n, lambda copy: copy.wait_send())
        if n == HEADS:
            pl.when(holder)(functools.partial(finish, n))
        else:
            finish(n)


def body(queries, keys, values, img_height, img_width, norm_gain, norm_bias):
    count = lax.axis_size("seq")
    features = norm_gain.shape[0]
    ends = jnp.cumsum(img_height * img_width)
    packed = ends * 64 + (32 - img_width)
    pad = -ends.shape[0] % HEAD
    slots = jnp.pad(
        jnp.stack([ends, packed]), ((0, 0), (0, pad)), constant_values=1 << 30
    ).reshape(2, -1, HEAD)
    dma = pltpu.SemaphoreType.DMA
    anywhere = pl.BlockSpec(memory_space=pl.ANY)
    resident = pl.BlockSpec(memory_space=pltpu.VMEM)
    stages = HEADS + 1
    return pl.pallas_call(
        functools.partial(kernel, count),
        out_shape=jax.ShapeDtypeStruct((MERGED, features), jnp.bfloat16),
        in_specs=[resident, anywhere, anywhere, anywhere, resident, resident],
        out_specs=resident,
        scratch_shapes=[
            pltpu.VMEM((stages, KROWS, HEAD), jnp.bfloat16),
            pltpu.VMEM((stages, KROWS, HEAD), jnp.bfloat16),
            pltpu.VMEM((stages, QROWS, HEAD), jnp.bfloat16),
            pltpu.VMEM((stages, SPAN, HEAD), jnp.bfloat16),
            pltpu.VMEM((ALL_HEADS, ROWS, HEAD), jnp.bfloat16),
            pltpu.VMEM((SPAN, HEAD), jnp.int32),
            pltpu.VMEM((SPAN, WINDOW), jnp.float32),
            pltpu.VMEM((ROWS, WINDOW), jnp.float32),
            pltpu.VMEM((ROWS, WINDOW), jnp.float32),
            pltpu.VMEM((ROWS, HEAD), jnp.float32),
            pltpu.VMEM((ROWS, HEAD), jnp.float32),
            dma((stages, 3, GROUP)), dma((stages, 3, GROUP)), dma((stages, 3)),
            dma((stages, 3, GROUP)), dma((stages, 3, GROUP)),
            dma((stages, GROUP)), dma((stages, GROUP)),
        ],
        compiler_params=pltpu.CompilerParams(
            collective_id=0, has_side_effects=True, vmem_limit_bytes=60 * 1024 * 1024
        ),
        name="packed_attention",
    )(
        slots, keys, values, queries,
        norm_gain.reshape(-1, HEAD), norm_bias.reshape(-1, HEAD),
    )


def solution(mesh):
    in_specs = (P("seq", None), P("seq", None), P("seq", None), P(), P(), P(), P())
    out_specs = P("seq", None)
    return jax.shard_map(body, mesh=mesh, in_specs=in_specs, out_specs=out_specs, check_vma=False)
```
